256 devices in a mesh: pipe: 4 (over x), seq: 64 (over y, z, core).
Axes of the slice: x: 4, y: 4, z: 8, core: 2. Of those that a mesh axis runs over, the one named last changes fastest.
Arguments:
- inputs: bfloat16 [4, 8192, 2048], P('pipe', 'seq'), may hold values from -6 to 6
- lengths: int32 [4, 256], replicated, may hold values from 1 to 128, 8192 in all within a row
- order: int32 [4], replicated, may hold values from 0 to 3, each once
- norm_gain: float32 [4, 2048], P('pipe'), may hold values from 0.25 to 1.75
- rate: float32 [4, 16, 2048], P('pipe'), may hold values from 0.004 to 0.15
- angle: float32 [4, 16, 2048], P('pipe'), may hold values from -3.140625 to 3.140625
- coef: float32 [4, 2, 16, 2048], P('pipe'), may hold values from -0.3 to 0.3
- skip: float32 [4, 2048], P('pipe'), may hold values from 0.5 to 1.5
- score_gains: float32 [4, 2, 2048], P('pipe'), may hold values from -3 to 4.6
- out_proj: bfloat16 [4, 2048, 2048], P('pipe', 'seq'), may hold values from -0.125 to 0.125
Outputs:
- outputs: bfloat16 [4, 8192, 2048], P('pipe', 'seq')
The draws below stay inside these ranges and needn't reach their ends.
Inputs may be any that keep to these rules, and one draw needn't show every extreme that they name: Each row of lengths sums to 8192, and every row holds a document of exactly 128 positions. `order`: each packed row appears once.
All inputs are finite; a program needn't handle non-finite values.
Results may differ from the reference program's by a relative error of at most 0.02.
The reference program's roundings to bfloat16 on the way count: a program that leaves them out, or rounds other values in their place, can miss the bound.
Values may be sent and summed in bfloat16 or wider, within the bound.
A program may use at most 128 MiB of HBM per device.

```python
import math
import jax
import jax.numpy as jnp
import numpy as np
from jax import lax

D = 2048
HEAD_DIM = 128
MODES = 16
TOK_DEV = 128
SECTIONS = 4
MICRO = 4
TOKENS = 8192
DOCS = 256


def draw_score_gains(key, part):
    head_count = D // HEAD_DIM
    keys_all = jax.random.split(jax.random.fold_in(key, 17), 5)
    section_keys = jax.random.split(keys_all[0], SECTIONS)
    ranks = jax.vmap(lambda one_key: jax.random.permutation(one_key, head_count))(section_keys)
    spread_heads = (ranks < head_count // 2).astype(jnp.float32)
    spread_mask = jnp.repeat(spread_heads, HEAD_DIM, axis=1)
    flips = jax.random.bernoulli(keys_all[1], 0.5, (SECTIONS, D))
    signs = jnp.where(flips, 1.0, -1.0).astype(jnp.float32)
    sign_pair = jnp.stack([signs, jnp.ones_like(signs)], axis=1)
    aligned = jax.random.uniform(keys_all[2], (SECTIONS, 2, D), jnp.float32, 0.6, 1.6)
    magnitude = jax.random.uniform(keys_all[4], (SECTIONS, 2, D), jnp.float32, 1.2, 2.4)
    spread_gain = magnitude * sign_pair
    return jnp.where(spread_mask[:, None, :] > 0.5, spread_gain, aligned)


def shard_levels(stream_key, shape, pieces, low, high):
    factor_of = 1.0
    for position, blocks in pieces:
        steps = jax.random.uniform(jax.random.fold_in(jax.random.fold_in(stream_key, 6), position), (blocks,), jnp.float32, low / len(pieces), high / len(pieces))
        factor_of = factor_of * jnp.repeat(jnp.exp(steps), shape[position] // blocks).reshape((-1,) + (1,) * (len(shape) - 1 - position))
    return factor_of


def profile(amount, total, limit, lean):
    portions = [(1 << 20) // math.isqrt(standing ** lean) + 1 for standing in range(2, amount + 1)]
    spare, given = total - limit - (amount - 1), [1] * (amount - 1)
    while spare > 0:
        candidates = [i for i in range(amount - 1) if given[i] < limit]
        whole, budget = sum([portions[i] for i in candidates]), spare
        for i in candidates:
            more = min(limit - given[i], max(1, budget * portions[i] // whole), spare)
            given[i] = given[i] + more
            spare = spare - more
    return np.array([limit] + given)


def ragged(key, amount, total, limit, slope):
    if amount == 2:
        one = jax.random.randint(key, (), max(1, total - limit), min(limit, total - 1) + 1)
        return jnp.stack([one, total - one])
    sizes = jnp.asarray(profile(amount, total, limit, slope), jnp.int32)
    couples = (amount - 1) // 2
    giver, taker = sizes[1:1 + 2 * couples:2], sizes[2:2 + 2 * couples:2]
    slack = jnp.minimum(giver - 1, limit - taker)
    passed = jax.random.randint(jax.random.fold_in(key, 1), (couples,), 0, 1 << 20) % (slack + 1)
    sizes = sizes.at[1:1 + 2 * couples:2].set(giver - passed).at[2:2 + 2 * couples:2].set(taker + passed)
    return sizes[jax.random.permutation(jax.random.fold_in(key, 2), amount)]


def gaussian(own_key, extent, deviation, most, cuts=(), kind=jnp.bfloat16):
    loudness = shard_levels(own_key, extent, cuts, -0.22, 0.18) if cuts else 1.0
    entries = jax.random.normal(own_key, extent, jnp.float32) * deviation * loudness
    return jnp.minimum(jnp.maximum(entries, -most), most).astype(kind)


def setup_inputs(seed: int = 0) -> dict:
    keys = jax.random.split(jax.random.key(seed), 11)
    inputs = gaussian(keys[0], (MICRO, TOKENS, D), 1.0, 6.0, ((0, 4), (1, 64)))
    lengths = jax.vmap(lambda own: ragged(own, DOCS, TOKENS, TOK_DEV, 2))(jax.random.split(keys[1], MICRO)).reshape((MICRO, DOCS)).astype(jnp.int32)
    order = jax.random.permutation(keys[2], MICRO).astype(jnp.int32)
    norm_gain = jnp.clip(1.0 + 0.15 * jax.random.normal(keys[3], (SECTIONS, D), jnp.float32), 0.25, 1.75)
    rate = jnp.clip(jnp.exp(math.log(0.15) - 3.624341 * jax.random.uniform(keys[4], (SECTIONS, MODES, D), jnp.float32) ** shard_levels(keys[4], (SECTIONS, MODES, D), ((0, 4),), -0.2, 0.2)), 0.004, 0.15)
    angle = jnp.clip(jax.random.uniform(keys[5], (SECTIONS, MODES, D), jnp.float32, -3.140625, 3.140625), -3.140625, 3.140625)
    coef = gaussian(keys[6], (SECTIONS, 2, MODES, D), 0.05, 0.3, ((0, 4),), jnp.float32)
    skip = jnp.clip(0.5 + 1.0 * jax.random.uniform(keys[7], (SECTIONS, D), jnp.float32) ** shard_levels(keys[7], (SECTIONS, D), ((0, 4),), -0.2, 0.2), 0.5, 1.5)
    score_gains = draw_score_gains(jax.random.fold_in(keys[10], 71), 0)
    out_proj = gaussian(keys[9], (SECTIONS, D, D), D ** -0.5, 0.125, ((0, 4), (1, 64)))
    return dict(inputs=inputs, lengths=lengths, order=order, norm_gain=norm_gain, rate=rate, angle=angle, coef=coef, skip=skip, score_gains=score_gains, out_proj=out_proj)


inner_span = 16
norm_eps = 1e-06
masked_score = -1e+30
highest = lax.Precision.HIGHEST

def mode_powers(rate_now, angle_now, exponents):
    magnitude = jnp.exp(-exponents[:, None, None] * rate_now[None])
    turning = exponents[:, None, None] * angle_now[None]
    return (magnitude * jnp.cos(turning), magnitude * jnp.sin(turning))

def mode_tables(rate_now, angle_now, coef_now):
    lag_steps = jnp.arange(inner_span).astype(jnp.float32)
    coef_re = coef_now[0]
    coef_im = coef_now[1]
    power_re, power_im = mode_powers(rate_now, angle_now, lag_steps)
    kernel = 2.0 * lax.optimization_barrier(jnp.sum(coef_re[None] * power_re - coef_im[None] * power_im, axis=1))
    ahead_re, ahead_im = mode_powers(rate_now, angle_now, lag_steps + 1.0)
    carry_re = coef_re[None] * ahead_re - coef_im[None] * ahead_im
    carry_im = coef_re[None] * ahead_im + coef_im[None] * ahead_re
    back_re, back_im = mode_powers(rate_now, angle_now, inner_span - 1.0 - lag_steps)
    whole_re, whole_im = mode_powers(rate_now, angle_now, jnp.full((1,), 1.0 * inner_span, jnp.float32))
    return (kernel, carry_re, carry_im, back_re, back_im, whole_re[0], whole_im[0])

def local_conv(kernel, signal, doc_ids):
    result = kernel[0][None, None, :] * signal
    for lag_steps in range(1, inner_span):
        shifted = jnp.pad(signal[:, :-lag_steps], ((0, 0), (lag_steps, 0), (0, 0)))
        same_doc = jnp.pad(doc_ids[:, lag_steps:] == doc_ids[:, :-lag_steps], ((0, 0), (lag_steps, 0)))
        result = result + kernel[lag_steps][None, None, :] * shifted * same_doc[:, :, None].astype(shifted.dtype)
    return result

def rms_scaled(values):
    return values * lax.rsqrt(lax.optimization_barrier(jnp.mean(values * values, axis=1, keepdims=True)) + norm_eps)

def ssm_mix(scaled, doc_ids, tables_all, skip_now):
    kernel, carry_re, carry_im, back_re, back_im, whole_re, whole_im = tables_all
    block_count = scaled.shape[0] // inner_span
    blocks = scaled.reshape(block_count, inner_span, scaled.shape[1])
    block_docs = doc_ids.reshape(block_count, inner_span)
    prior_docs = jnp.concatenate([jnp.full((1,), -1, jnp.int32), block_docs[:-1, -1].astype(jnp.int32)])
    base_out = local_conv(kernel, blocks, block_docs) + skip_now * blocks

    def advance(carried, item):
        state_re, state_im = carried
        block_now, docs_now, prior_now = item
        entry_flags = (docs_now == prior_now).astype(block_now.dtype)
        reached = 2.0 * (jnp.einsum('tmd,md->td', carry_re, state_re, precision=highest) - jnp.einsum('tmd,md->td', carry_im, state_im, precision=highest))
        last_doc = docs_now[-1]
        kept_rows = block_now * (docs_now == last_doc).astype(block_now.dtype)[:, None]
        local_re = jnp.einsum('smd,sd->md', back_re, kept_rows, precision=highest)
        local_im = jnp.einsum('smd,sd->md', back_im, kept_rows, precision=highest)
        link_now = (last_doc == prior_now).astype(block_now.dtype)
        next_re = local_re + link_now * (whole_re * state_re - whole_im * state_im)
        next_im = local_im + link_now * (whole_re * state_im + whole_im * state_re)
        return ((next_re, next_im), entry_flags[:, None] * reached)
    zeros = jnp.zeros(whole_re.shape, jnp.float32)
    _, reached_all = lax.scan(advance, (zeros, zeros), (blocks, block_docs, prior_docs))
    return (base_out + reached_all).reshape(scaled.shape)

def block_attention(query_rows, key_rows, value_rows, residual, query_docs, key_docs, query_pos, key_pos, proj_now):
    row_count = query_rows.shape[0]
    query_heads = query_rows.astype(jnp.float32).reshape(row_count, -1, HEAD_DIM)
    key_heads = key_rows.astype(jnp.float32).reshape(key_rows.shape[0], -1, HEAD_DIM)
    value_heads = value_rows.astype(jnp.float32).reshape(value_rows.shape[0], -1, HEAD_DIM)
    scores = jnp.einsum('thd,shd->hts', query_heads, key_heads, precision=highest) * HEAD_DIM ** (-0.5)
    allowed = (key_pos[None, :] <= query_pos[:, None]) & (key_docs[None, :] == query_docs[:, None])
    scores = jnp.where(allowed[None], scores, masked_score)
    largest = lax.optimization_barrier(jnp.max(scores, axis=2, keepdims=True))
    raw_weights = jnp.exp(scores - largest)
    weights = (raw_weights / lax.optimization_barrier(jnp.sum(raw_weights, axis=2, keepdims=True))).astype(jnp.bfloat16)
    attended = jnp.einsum('hts,shd->thd', weights.astype(jnp.float32), value_heads, precision=highest)
    attended = attended.reshape(row_count, -1).astype(jnp.bfloat16)
    projected = jnp.dot(attended, proj_now, preferred_element_type=jnp.float32)
    return (residual.astype(jnp.float32) + projected).astype(jnp.bfloat16)

def doc_attention(middle, doc_ids, gains_now, proj_now):
    total_rows = middle.shape[0]
    normed = rms_scaled(middle.astype(jnp.float32))
    queries = (normed * gains_now[0]).astype(jnp.bfloat16)
    key_rows = (normed * gains_now[1]).astype(jnp.bfloat16)
    padding = jnp.zeros((TOK_DEV, middle.shape[1]), jnp.bfloat16)
    keys_padded = jnp.concatenate([padding, key_rows])
    values_padded = jnp.concatenate([padding, middle])
    docs_padded = jnp.concatenate([jnp.full((TOK_DEV,), -1, jnp.int32), doc_ids.astype(jnp.int32)])
    pos_padded = (jnp.arange(total_rows + TOK_DEV) - TOK_DEV).astype(jnp.int32)

    def one_block(index):
        first = (index * TOK_DEV).astype(jnp.int32)
        own_first = (first + TOK_DEV).astype(jnp.int32)
        query_rows = lax.dynamic_slice_in_dim(queries, first, TOK_DEV, 0)
        residual = lax.dynamic_slice_in_dim(middle, first, TOK_DEV, 0)
        key_now = lax.dynamic_slice_in_dim(keys_padded, first, 2 * TOK_DEV, 0)
        value_now = lax.dynamic_slice_in_dim(values_padded, first, 2 * TOK_DEV, 0)
        key_docs = lax.dynamic_slice_in_dim(docs_padded, first, 2 * TOK_DEV, 0)
        key_pos = lax.dynamic_slice_in_dim(pos_padded, first, 2 * TOK_DEV, 0)
        query_docs = lax.dynamic_slice_in_dim(docs_padded, own_first, TOK_DEV, 0)
        query_pos = lax.dynamic_slice_in_dim(pos_padded, own_first, TOK_DEV, 0)
        return block_attention(query_rows, key_now, value_now, residual, query_docs, key_docs, query_pos, key_pos, proj_now)
    results = lax.map(one_block, jnp.arange(total_rows // TOK_DEV).astype(jnp.int32))
    return results.reshape(total_rows, middle.shape[1])

def reference(inputs, lengths, order, norm_gain, rate, angle, coef, skip, score_gains, out_proj):
    total_rows = inputs.shape[1]
    positions = jnp.arange(total_rows).astype(jnp.int32)
    finished = []
    for slot_index in range(inputs.shape[0]):
        chosen = order[slot_index]
        current = inputs[chosen]
        doc_ends = jnp.cumsum(lengths[chosen]).astype(jnp.int32)
        doc_ids = lax.optimization_barrier(jnp.sum((doc_ends[None, :] <= positions[:, None]).astype(jnp.int32), axis=1)).astype(jnp.int32)
        for section_index in range(norm_gain.shape[0]):
            tables_all = mode_tables(rate[section_index], angle[section_index], coef[section_index])
            plain = current.astype(jnp.float32)
            scaled = rms_scaled(plain) * norm_gain[section_index]
            mixed = ssm_mix(scaled, doc_ids, tables_all, skip[section_index])
            middle = (plain + mixed).astype(jnp.bfloat16)
            current = doc_attention(middle, doc_ids, score_gains[section_index], out_proj[section_index])
        finished.append(current)
    return jnp.stack(finished)
```

```python
import functools

import jax
import jax.numpy as jnp
from jax import lax
from jax.experimental import pallas as pl
from jax.experimental.pallas import tpu as pltpu
from jax.sharding import PartitionSpec as P

HEAD_DIM = 128
LANES = 128
norm_eps = 1e-06
masked_score = -1e30


MESH = pl.DeviceIdType.MESH
ZS, YS, XS = 8, 4, 4


class Mover:
    def __init__(self, send_sems, recv_sems):
        self.send_sems, self.recv_sems, self.used, self.open = send_sems, recv_sems, 0, []

    def push(self, source, target, incoming, device):
        k = self.used
        self.used += 1
        out = pltpu.make_async_remote_copy(source, target, self.send_sems.at[k], self.recv_sems.at[k],
                                           device_id=device, device_id_type=MESH)
        out.start()
        back = pltpu.make_async_remote_copy(incoming, incoming, self.send_sems.at[k], self.recv_sems.at[k],
                                            device_id=device, device_id_type=MESH)
        self.open.append(out)
        return back.wait_recv

    def finish(self):
        for out in self.open:
            out.wait_send()
        self.open = []


def ring(mover, size, me, block, half, device):
    def at(shift):
        return lax.rem(me + (shift + size), size)
    waits = {}

    def step(t):
        def go():
            if t > 1:
                waits[t - 1, 0]()
                waits[t - 1, 1]()
            if t <= size // 2:
                pick = (lambda i, k: half(i, k)) if t == size // 2 else (lambda i, k: block(i))
                ahead, behind = at(1 - t), at(t - 1)
                waits[t, 0] = mover.push(pick(ahead, 0), pick(ahead, 0), pick(at(-t), 0), device(at(1)))
                waits[t, 1] = mover.push(pick(behind, 1), pick(behind, 1), pick(at(t), 1), device(at(-1)))
        return go
    return [step(t) for t in range(1, size // 2 + 2)]


def transfer_steps(mover, refs, chosen, width, split):
    w_ref, in_ref, tab_in, wg, xin, tabs, x, local_sem = refs
    pipe, seq = lax.axis_index("pipe"), lax.axis_index("seq")
    core, z, y = lax.rem(seq, 2), lax.rem(seq // 2, ZS), seq // (2 * ZS)
    rows = in_ref.shape[0]
    nseq = 2 * ZS * YS

    def seq_of(yy, zz, cc):
        return (yy * ZS + zz) * 2 + cc

    def to_x(i):
        return (i, seq)

    def to_y(i):
        return (pipe, seq_of(i, z, core))

    def to_z(i):
        return (pipe, seq_of(y, i, core))

    partner = (pipe, seq_of(y, z, 1 - core))
    following = (pipe, lax.rem(seq + 1, nseq))
    preceding = (pipe, lax.rem(seq + nseq - 1, nseq))
    peers = [to_x(lax.rem(pipe + 1, XS)), to_x(lax.rem(pipe + 3, XS)), to_y(lax.rem(y + 1, YS)), to_y(lax.rem(y + 3, YS)),
             to_z(lax.rem(z + 1, ZS)), to_z(lax.rem(z + 7, ZS)), partner, following, preceding]
    trows = tabs.shape[1] // 2
    tlow = pl.ds(core * trows, trows)
    tpart = [pl.ds(core * trows + k * (trows // 2), trows // 2) for k in range(2)]
    depth = w_ref.shape[0]

    def begin():
        bar = pltpu.get_barrier_semaphore()
        for peer in peers:
            pl.semaphore_signal(bar, inc=1, device_id=peer, device_id_type=MESH)
        pl.semaphore_wait(bar, len(peers))
        copies = [pltpu.make_async_copy(w_ref, wg.at[pipe, y, z, core], local_sem.at[0]),
                  pltpu.make_async_copy(in_ref, xin.at[pipe], local_sem.at[1]),
                  pltpu.make_async_copy(tab_in.at[tlow], tabs.at[pipe, tlow], local_sem.at[2])]
        for c in copies:
            c.start()
        for c in copies:
            c.wait()

    xw = ring(mover, XS, pipe, lambda i: wg.at[i, y, z, core],
              lambda i, k: wg.at[i, y, z, core, pl.ds(k * (depth // 2), depth // 2)], to_x)
    xi = ring(mover, XS, pipe, lambda i: xin.at[i], lambda i, k: xin.at[i, pl.ds(k * (rows // 2), rows // 2)], to_x)
    xt = ring(mover, XS, pipe, lambda i: tabs.at[i, tlow], lambda i, k: tabs.at[i, tpart[k]], to_x)
    ca, cb = pl.ds(0, split), pl.ds(split, width - split)
    pair = [pl.ds(0, XS // 2), pl.ds(XS // 2, XS // 2)]
    ya = ring(mover, YS, y, lambda i: wg.at[:, i, z, core, :, ca], lambda i, k: wg.at[pair[k], i, z, core, :, ca], to_y)
    zb = ring(mover, ZS, z, lambda i: wg.at[:, y, i, core, :, cb], lambda i, k: wg.at[pair[k], y, i, core, :, cb], to_z)
    held = {}

    def choose():
        x[pl.ds(rows, rows), :] = xin[chosen]
        held["halo"] = mover.push(x.at[pl.ds(rows, rows)], x.at[pl.ds(0, rows)], x.at[pl.ds(0, rows)], following)

    def share_tables():
        other = pl.ds((1 - core) * trows, trows)
        held["tabs"] = mover.push(tabs.at[:, tlow], tabs.at[:, tlow], tabs.at[:, other], partner)

    def last(s):
        yh = [pl.ds(0, YS // 2), pl.ds(YS // 2, YS // 2)]
        zh = [pl.ds(0, ZS // 2), pl.ds(ZS // 2, ZS // 2)]
        za = ring(mover, ZS, z, lambda i: wg.at[s, :, i, core, :, ca], lambda i, k: wg.at[s, yh[k], i, core, :, ca], to_z)
        yb = ring(mover, YS, y, lambda i: wg.at[s, i, :, core, :, cb], lambda i, k: wg.at[s, i, zh[k], core, :, cb], to_y)
        return za, yb

    def swap(s):
        held["w", s] = mover.push(wg.at[s, :, :, core], wg.at[s, :, :, core], wg.at[s, :, :, 1 - core], partner)

    finals = [last(s) for s in range(XS)]
    early = [begin, xw[0], xw[1], xi[0], xw[2], ya[0], zb[0], xt[0], zb[1], ya[1], xi[1], zb[2], ya[2], zb[3], xt[1], xi[2], choose,
             xt[2], share_tables, zb[4]]
    wait_inputs = [lambda: held["halo"](), lambda: held["tabs"]()]
    per_section = []
    for s in range(XS):
        za, yb = finals[s]
        steps = [] if s else [za[0], yb[0]]
        steps += [za[1], za[2], yb[1], za[3]]
        if s + 1 < XS:
            steps += [finals[s + 1][0][0], finals[s + 1][1][0]]
        steps += [za[4], yb[2], functools.partial(swap, s)]
        per_section.append((steps, (lambda s=s: held["w", s]())))
    return early, wait_inputs, per_section


def comm_kernel(width, split, order_ref, w_ref, in_ref, tab_in, wg, tabs, x, xin, send_sems, recv_sems, local_sem):
    mover = Mover(send_sems, recv_sems)
    chosen = order_ref[lax.axis_index("pipe")]
    early, wait_inputs, per_section = transfer_steps(
        mover, (w_ref, in_ref, tab_in, wg, xin, tabs, x, local_sem), chosen, width, split)
    for step in early + wait_inputs:
        step()
    for steps, done in per_section:
        for step in steps:
            step()
    for steps, done in per_section:
        done()
    mover.finish()


def compute_kernel(sections, modes, rows, width, x_ref, link_ref, docq_ref, dock_ref, tab_ref, w_hbm, o_ref,
                   cur, xs, ys, mid, qs, ks, att, bias, wbuf, wsem):
    groups = width // LANES
    halves = groups // 8
    own = rows // 2
    f32, bf16 = jnp.float32, jnp.bfloat16

    def fetch(s, slot):
        return pltpu.make_async_copy(w_hbm.at[s], wbuf.at[slot], wsem.at[slot])

    fetch(0, 0).start()
    cur[...] = x_ref[...]
    qpos = lax.broadcasted_iota(jnp.int32, (own, rows), 0) + own
    kpos = lax.broadcasted_iota(jnp.int32, (own, rows), 1)
    for half in range(2):
        good = (docq_ref[half * own:(half + 1) * own, :] == dock_ref[...]) & (kpos <= qpos - (1 - half) * own)
        bias[half * own:(half + 1) * own, :] = jnp.where(good, 0.0, masked_score)

    def section(s, carry):
        slot = s % 2

        @pl.when(s + 1 < sections)
        def _():
            fetch(s + 1, 1 - slot).start()

        def spread(r, c):
            base = pl.multiple_of(r * 16, 16)
            xb = cur[pl.ds(base, 16), :].astype(f32)
            inv = lax.rsqrt(jnp.mean(xb * xb, axis=1, keepdims=True) + norm_eps)
            for g in range(groups):
                sc = xb[:, g * LANES:(g + 1) * LANES] * inv * tab_ref[s, 4 * modes, g:g + 1, :]
                for h in range(2):
                    xs[pl.ds((base + 8 * h) * groups + g, 8, stride=groups), :] = sc[8 * h:8 * h + 8]
            return c

        lax.fori_loop(0, rows // 16, spread, 0)

        per = 8
        for hf in range(halves):
            for mg in range(modes // per):
                c1 = [tab_ref[s, mg * per + m, 8 * hf:8 * hf + 8, :] for m in range(per)]
                c2 = [tab_ref[s, modes + mg * per + m, 8 * hf:8 * hf + 8, :] for m in range(per)]
                b0 = [tab_ref[s, 2 * modes + mg * per + m, 8 * hf:8 * hf + 8, :] for m in range(per)]
                b1 = [tab_ref[s, 3 * modes + mg * per + m, 8 * hf:8 * hf + 8, :] for m in range(per)]
                skip = tab_ref[s, 4 * modes + 1, 8 * hf:8 * hf + 8, :]

                def step(p0, state, c1=c1, c2=c2, b0=b0, b1=b1, skip=skip, hf=hf, mg=mg):
                    w1, w2 = list(state[:per]), list(state[per:])
                    for u in range(4):
                        p = p0 * 4 + u
                        at = pl.multiple_of(p * groups + 8 * hf, 8)
                        x = xs[pl.ds(at, 8), :]
                        link = link_ref[0, p]
                        acc = skip * x if mg == 0 else ys[pl.ds(at, 8), :]
                        parts = []
                        for m in range(per):
                            k1 = w1[m] * link
                            k2 = w2[m] * link
                            w = x + (c1[m] * k1 + c2[m] * k2)
                            parts.append(b0[m] * w + b1[m] * k1)
                            w1[m], w2[m] = w, k1
                        while len(parts) > 1:
                            parts = [parts[i] + parts[i + 1] for i in range(0, len(parts), 2)]
                        ys[pl.ds(at, 8), :] = acc + parts[0]
                    return tuple(w1) + tuple(w2)

                zero = jnp.zeros((8, LANES), f32)
                lax.fori_loop(0, rows // 4, step, (zero,) * (2 * per))

        def gather(r, c):
            base = pl.multiple_of(r * 16, 16)
            sq = jnp.zeros((16, LANES), f32)
            mids = []
            for g in range(groups):
                mixed = jnp.concatenate(
                    [ys[pl.ds((base + 8 * h) * groups + g, 8, stride=groups), :] for h in range(2)], axis=0)
                mb = (cur[pl.ds(base, 16), g * LANES:(g + 1) * LANES].astype(f32) + mixed).astype(bf16)
                mid[pl.ds(base, 16), g * LANES:(g + 1) * LANES] = mb
                mf = mb.astype(f32)
                sq = sq + mf * mf
            inv = lax.rsqrt(jnp.sum(sq, axis=1, keepdims=True) * (1.0 / width) + norm_eps)
            for g in range(groups):
                lanes = slice(g * LANES, (g + 1) * LANES)
                normed = mid[pl.ds(base, 16), lanes].astype(f32) * inv
                qs[pl.ds(base, 16), lanes] = (normed * tab_ref[s, 4 * modes + 2, g:g + 1, :]).astype(bf16)
                ks[pl.ds(base, 16), lanes] = (normed * tab_ref[s, 4 * modes + 3, g:g + 1, :]).astype(bf16)
            return c

        lax.fori_loop(0, rows // 16, gather, 0)

        def head(h, c):
            lanes = pl.ds(pl.multiple_of(h * HEAD_DIM, HEAD_DIM), HEAD_DIM)
            for half in range(2):
                qrows = slice(half * own, (half + 1) * own)
                krows = slice(0, (half + 1) * own)
                scores = lax.dot_general(qs[qrows, lanes], ks[krows, lanes], (((1,), (1,)), ((), ())),
                                         preferred_element_type=f32) * HEAD_DIM ** (-0.5)
                scores = scores + bias[qrows, krows]
                largest = jnp.max(scores, axis=1, keepdims=True)
                raw = jnp.exp(scores - largest)
                weights = (raw / jnp.sum(raw, axis=1, keepdims=True)).astype(bf16)
                att[qrows, lanes] = jnp.dot(weights, mid[krows, lanes], preferred_element_type=f32).astype(bf16)
            return c

        lax.fori_loop(0, width // HEAD_DIM, head, 0)

        fetch(s, slot).wait()
        cols = 256

        def project(n, c):
            lanes = pl.ds(pl.multiple_of(n * cols, cols), cols)
            acc = jnp.dot(att[...], wbuf[slot, :, lanes], preferred_element_type=f32)
            cur[:, lanes] = (mid[:, lanes].astype(f32) + acc).astype(bf16)
            return c

        lax.fori_loop(0, width // cols, project, 0)
        return carry

    lax.fori_loop(0, sections, section, 0)
    o_ref[...] = cur[own:, :]


def mode_table(rate, angle, coef, norm_gain, skip, gains):
    mag = jnp.exp(-rate)
    a_re, a_im = mag * jnp.cos(angle), mag * jnp.sin(angle)
    c1 = 2.0 * a_re
    c2 = -(mag * mag)
    b0 = 2.0 * coef[0]
    b1 = -2.0 * (coef[0] * a_re + coef[1] * a_im)
    return jnp.concatenate([c1, c2, b0, b1, norm_gain[None], skip[None], gains], axis=0)


def local(inputs, lengths, order, norm_gain, rate, angle, coef, skip, score_gains, out_proj):
    sections = lax.axis_size("pipe")
    seqs = lax.axis_size("seq")
    pipe = lax.axis_index("pipe")
    seq = lax.axis_index("seq")
    rows, width = inputs.shape[1], inputs.shape[2]
    modes = rate.shape[1]
    groups = width // LANES
    table = mode_table(rate[0], angle[0], coef[0], norm_gain[0], skip[0], score_gains[0]).reshape(-1, groups, LANES)
    vm = pl.BlockSpec(memory_space=pltpu.VMEM)
    sm = pl.BlockSpec(memory_space=pltpu.SMEM)
    hb = pl.BlockSpec(memory_space=pl.ANY)
    total = 2 * rows
    moves = 82
    whole, tabs, x = pl.pallas_call(
        functools.partial(comm_kernel, width, 896),
        out_shape=(jax.ShapeDtypeStruct((sections, YS, ZS, 2, out_proj.shape[1], width), jnp.bfloat16),
                   jax.ShapeDtypeStruct((sections,) + table.shape, jnp.float32),
                   jax.ShapeDtypeStruct((total, width), jnp.bfloat16)),
        in_specs=[sm, hb, hb, hb],
        out_specs=(hb, vm, vm),
        scratch_shapes=[
            pltpu.VMEM((sections, rows, width), jnp.bfloat16),
            pltpu.SemaphoreType.DMA((moves,)),
            pltpu.SemaphoreType.DMA((moves,)),
            pltpu.SemaphoreType.DMA((3,)),
        ],
        compiler_params=pltpu.CompilerParams(collective_id=0, has_side_effects=True, vmem_limit_bytes=32 << 20),
        name="exchange",
    )(order, out_proj[0], inputs[0], table)
    whole = whole.reshape(sections, width, width)

    chosen = lax.dynamic_index_in_dim(order, pipe, 0, False)
    positions = seq * rows - rows + jnp.arange(2 * rows)
    doc_ends = jnp.cumsum(lax.dynamic_index_in_dim(lengths, chosen, 0, False))
    counted = jnp.sum((doc_ends[None, :] <= positions[:, None]).astype(jnp.int32), axis=1)
    docs = jnp.where(positions >= 0, counted, -1)
    link = jnp.concatenate([jnp.zeros((1,), jnp.float32), (docs[1:] == docs[:-1]).astype(jnp.float32)])

    out = pl.pallas_call(
        functools.partial(compute_kernel, sections, modes, total, width),
        out_shape=jax.ShapeDtypeStruct((rows, width), jnp.bfloat16),
        in_specs=[vm, sm, vm, vm, vm, hb],
        out_specs=vm,
        scratch_shapes=[
            pltpu.VMEM((total, width), jnp.bfloat16),
            pltpu.VMEM((total * groups, LANES), jnp.float32),
            pltpu.VMEM((total * groups, LANES), jnp.float32),
            pltpu.VMEM((total, width), jnp.bfloat16),
            pltpu.VMEM((total, width), jnp.bfloat16),
            pltpu.VMEM((total, width), jnp.bfloat16),
            pltpu.VMEM((total, width), jnp.bfloat16),
            pltpu.VMEM((total, total), jnp.float32),
            pltpu.VMEM((2, width, width), jnp.bfloat16),
            pltpu.SemaphoreType.DMA((2,)),
        ],
        compiler_params=pltpu.CompilerParams(vmem_limit_bytes=56 << 20),
        name="sections",
    )(x, link[None], docs[:, None], docs[None, :], tabs, whole)
    return out[None]


def solution(mesh):
    in_specs = (
        P("pipe", "seq", None),
        P(),
        P(),
        P("pipe", None),
        P("pipe", None, None),
        P("pipe", None, None),
        P("pipe", None, None, None),
        P("pipe", None),
        P("pipe", None, None),
        P("pipe", "seq", None),
    )
    out_specs = P("pipe", "seq", None)
    return jax.shard_map(local, mesh=mesh, in_specs=in_specs, out_specs=out_specs, check_vma=False)
```

```python
import functools

import jax
import jax.numpy as jnp
from jax import lax
from jax.experimental import pallas as pl
from jax.experimental.pallas import tpu as pltpu
from jax.sharding import PartitionSpec as P

HEAD_DIM = 128
LANES = 128
norm_eps = 1e-06
masked_score = -1e30


MESH = pl.DeviceIdType.MESH
ZS, YS, XS = 8, 4, 4


class Mover:
    def __init__(self, send_sems, recv_sems):
        self.send_sems, self.recv_sems, self.used, self.open = send_sems, recv_sems, 0, []

    def push(self, source, target, incoming, device):
        k = self.used
        self.used += 1
        out = pltpu.make_async_remote_copy(source, target, self.send_sems.at[k], self.recv_sems.at[k],
                                           device_id=device, device_id_type=MESH)
        out.start()
        back = pltpu.make_async_remote_copy(incoming, incoming, self.send_sems.at[k], self.recv_sems.at[k],
                                            device_id=device, device_id_type=MESH)
        self.open.append(out)
        return back.wait_recv

    def finish(self):
        for out in self.open:
            out.wait_send()
        self.open = []


def ring(mover, size, me, block, half, device, share=None):
    def at(shift):
        return lax.rem(me + (shift + size), size)
    waits = {}

    def step(t):
        def go():
            if t > 1:
                waits[t - 1, 0]()
                waits[t - 1, 1]()
            if t <= size // 2:
                pick = (lambda i, k: half(i, k)) if t == size // 2 else (lambda i, k: block(i))
                ahead, behind = at(1 - t), at(t - 1)
                waits[t, 0] = mover.push(pick(ahead, 0), pick(ahead, 0), pick(at(-t), 0), device(at(1)))
                waits[t, 1] = mover.push(pick(behind, 1), pick(behind, 1), pick(at(t), 1), device(at(-1)))
            if share is not None:
                share(at(t - 1))
                if 1 < t <= size // 2:
                    share(at(1 - t))
        return go
    return [step(t) for t in range(1, size // 2 + 2)]


def transfer_steps(mover, refs, chosen, width, split):
    w_ref, in_ref, tab_in, wg, xin, tabs, x, local_sem = refs
    pipe, seq = lax.axis_index("pipe"), lax.axis_index("seq")
    core, z, y = lax.rem(seq, 2), lax.rem(seq // 2, ZS), seq // (2 * ZS)
    rows = in_ref.shape[0]
    nseq = 2 * ZS * YS

    def seq_of(yy, zz, cc):
        return (yy * ZS + zz) * 2 + cc

    def to_x(i):
        return (i, seq)

    def to_y(i):
        return (pipe, seq_of(i, z, core))

    def to_z(i):
        return (pipe, seq_of(y, i, core))

    partner = (pipe, seq_of(y, z, 1 - core))
    following = (pipe, lax.rem(seq + 1, nseq))
    preceding = (pipe, lax.rem(seq + nseq - 1, nseq))
    peers = [to_x(lax.rem(pipe + 1, XS)), to_x(lax.rem(pipe + 3, XS)), to_y(lax.rem(y + 1, YS)), to_y(lax.rem(y + 3, YS)),
             to_z(lax.rem(z + 1, ZS)), to_z(lax.rem(z + 7, ZS)), partner, following, preceding]
    trows = tabs.shape[1] // 2
    tlow = pl.ds(core * trows, trows)
    tpart = [pl.ds(core * trows + k * (trows // 2), trows // 2) for k in range(2)]
    depth = w_ref.shape[0]

    def begin():
        bar = pltpu.get_barrier_semaphore()
        for peer in peers:
            pl.semaphore_signal(bar, inc=1, device_id=peer, device_id_type=MESH)
        pl.semaphore_wait(bar, len(peers))
        copies = [pltpu.make_async_copy(w_ref, wg.at[pipe, y, z, core], local_sem.at[0]),
                  pltpu.make_async_copy(in_ref, xin.at[pipe], local_sem.at[1]),
                  pltpu.make_async_copy(tab_in.at[tlow], tabs.at[pipe, tlow], local_sem.at[2])]
        for c in copies:
            c.start()
        for c in copies:
            c.wait()

    xw = ring(mover, XS, pipe, lambda i: wg.at[i, y, z, core],
              lambda i, k: wg.at[i, y, z, core, pl.ds(k * (depth // 2), depth // 2)], to_x)
    xi = ring(mover, XS, pipe, lambda i: xin.at[i], lambda i, k: xin.at[i, pl.ds(k * (rows // 2), rows // 2)], to_x)
    xt = ring(mover, XS, pipe, lambda i: tabs.at[i, tlow], lambda i, k: tabs.at[i, tpart[k]], to_x)
    ca, cb = pl.ds(0, split), pl.ds(split, width - split)
    pair = [pl.ds(0, XS // 2), pl.ds(XS // 2, XS // 2)]
    ya = ring(mover, YS, y, lambda i: wg.at[:, i, z, core, :, ca], lambda i, k: wg.at[pair[k], i, z, core, :, ca], to_y)
    zb = ring(mover, ZS, z, lambda i: wg.at[:, y, i, core, :, cb], lambda i, k: wg.at[pair[k], y, i, core, :, cb], to_z)
    held = {}

    def choose():
        x[pl.ds(rows, rows), :] = xin[chosen]
        held["halo"] = mover.push(x.at[pl.ds(rows, rows)], x.at[pl.ds(0, rows)], x.at[pl.ds(0, rows)], following)

    def share_tables():
        other = pl.ds((1 - core) * trows, trows)
        held["tabs"] = mover.push(tabs.at[:, tlow], tabs.at[:, tlow], tabs.at[:, other], partner)

    shared = {s: [] for s in range(XS)}

    def last(s):
        yh = [pl.ds(0, YS // 2), pl.ds(YS // 2, YS // 2)]
        zh = [pl.ds(0, ZS // 2), pl.ds(ZS // 2, ZS // 2)]

        def to_partner(part):
            def share(i):
                shared[s].append(mover.push(part(i, core), part(i, core), part(i, 1 - core), partner))
            return share
        part_a = lambda i, c: wg.at[s, :, i, c, :, ca]
        part_b = lambda i, c: wg.at[s, i, :, c, :, cb]
        za = ring(mover, ZS, z, lambda i: part_a(i, core), lambda i, k: wg.at[s, yh[k], i, core, :, ca], to_z, to_partner(part_a))
        yb = ring(mover, YS, y, lambda i: part_b(i, core), lambda i, k: wg.at[s, i, zh[k], core, :, cb], to_y, to_partner(part_b))
        return za, yb

    finals = [last(s) for s in range(XS)]
    early = [begin, xw[0], xw[1], xi[0], xw[2], ya[0], zb[0], xt[0], zb[1], ya[1], xi[1], zb[2], ya[2], zb[3], xt[1], xi[2], choose,
             xt[2], share_tables, zb[4], finals[0][1][0], finals[0][0][0]]
    per_section = []
    for s in range(XS):
        za, yb = finals[s]
        steps = [za[1], za[2], yb[1], za[3]]
        if s + 1 < XS:
            steps += [lambda s=s: (finals[s + 1][1][0](), finals[s + 1][0][0]())]
        steps += [za[4], yb[2]]
        per_section.append(steps)

    def arrived(s):
        for wait in shared[s]:
            wait()
    return early, held, per_section, arrived


def document_masks(lengths_ref, chosen, first, rows, bias, links):
    f32, bf16 = jnp.float32, jnp.bfloat16
    count = lengths_ref.shape[1]
    own = rows // 2
    sizes = jnp.broadcast_to(lengths_ref[pl.ds(chosen, 1), :].astype(f32), (8, count)).astype(bf16)
    low = (lax.broadcasted_iota(jnp.int32, (count, count), 1) <= lax.broadcasted_iota(jnp.int32, (count, count), 0))
    low = low.astype(f32).astype(bf16)
    both = (((1,), (1,)), ((), ()))
    ends_row = lax.dot_general(sizes, low, both, preferred_element_type=f32)[0:1, :].astype(jnp.int32)
    ends_col = lax.dot_general(low, sizes, both, preferred_element_type=f32)[:, 0:1].astype(jnp.int32)
    index = lax.broadcasted_iota(jnp.int32, (rows, count), 0)
    down = index + first

    def doc_col(pos):
        counted = jnp.sum(jnp.where(ends_row <= pos, 1.0, 0.0), axis=1, keepdims=True)
        return jnp.where(pos[:, 0:1] >= 0, counted, -1.0)
    docs = doc_col(down)
    before = doc_col(down - 1)
    across = lax.broadcasted_iota(jnp.int32, (count, rows), 1) + first
    docs_row = jnp.sum(jnp.where(ends_col <= across, 1.0, 0.0), axis=0, keepdims=True)
    docs_row = jnp.where(across[0:1, :] >= 0, docs_row, -1.0)
    good = (docs == docs_row) & (lax.broadcasted_iota(jnp.int32, (rows, rows), 1) <= lax.broadcasted_iota(jnp.int32, (rows, rows), 0))
    bias[...] = jnp.where(good, 0.0, masked_score)
    link = jnp.where((docs == before) & (index[:, 0:1] > 0), 1.0, 0.0)
    wide = jnp.broadcast_to(link, (rows, LANES))
    for r in range(rows // 8):
        for j in range(8):
            links[pl.ds(r * 64 + j, 8, stride=8), :] = wide[r * 8:r * 8 + 8]


def fused_kernel(width, split, modes, order_ref, lengths_ref, w_ref, in_ref, tab_in, o_ref,
                 wg, tab_ref, cur, xin, xs, ys, mid, qs, ks, att, bias, links, send_sems, recv_sems, local_sem):
    sections = wg.shape[0]
    rows = cur.shape[0]
    groups = width // LANES
    halves = groups // 8
    own = rows // 2
    f32, bf16 = jnp.float32, jnp.bfloat16
    mover = Mover(send_sems, recv_sems)
    chosen = order_ref[lax.axis_index("pipe")]
    early, held, per_section, arrived = transfer_steps(
        mover, (w_ref, in_ref, tab_in, wg, xin, tab_ref, cur, local_sem), chosen, width, split)
    for k, step in enumerate(early):
        step()
        if k == 3:
            document_masks(lengths_ref, chosen, (lax.axis_index("seq") - 1) * own, rows, bias, links)
    held["halo"]()
    held["tabs"]()
    queue = []

    def serve(n=1):
        for _ in range(min(n, len(queue))):
            queue.pop(0)()

    for s in range(sections):
        queue += per_section[s]

        def spread(r, c, s=s):
            base = pl.multiple_of(r * 16, 16)
            xb = cur[pl.ds(base, 16), :].astype(f32)
            inv = lax.rsqrt(jnp.mean(xb * xb, axis=1, keepdims=True) + norm_eps)
            for g in range(groups):
                sc = xb[:, g * LANES:(g + 1) * LANES] * inv * tab_ref[s, 4 * modes, g:g + 1, :]
                for h in range(2):
                    xs[pl.ds((base + 8 * h) * groups + g, 8, stride=groups), :] = sc[8 * h:8 * h + 8]
            return c

        lax.fori_loop(0, rows // 16, spread, 0)
        serve()

        per = 8
        for hf in range(halves):
            for mg in range(modes // per):
                part = slice(8 * hf, 8 * hf + 8)
                c1 = [tab_ref[s, mg * per + m, part, :] for m in range(per)]
                c2 = [tab_ref[s, modes + mg * per + m, part, :] for m in range(per)]
                b0 = [tab_ref[s, 2 * modes + mg * per + m, part, :] for m in range(per)]
                b1 = [tab_ref[s, 3 * modes + mg * per + m, part, :] for m in range(per)]
                skip = tab_ref[s, 4 * modes + 1, part, :]

                def step(p0, state, c1=c1, c2=c2, b0=b0, b1=b1, skip=skip, hf=hf, mg=mg):
                    w1, w2 = list(state[:per]), list(state[per:])
                    for u in range(4):
                        p = p0 * 4 + u
                        at = pl.multiple_of(p * groups + 8 * hf, 8)
                        x = xs[pl.ds(at, 8), :]
                        link = links[pl.ds(pl.multiple_of(p * 8, 8), 8), :]
                        acc = skip * x if mg == 0 else ys[pl.ds(at, 8), :]
                        parts = []
                        for m in range(per):
                            k1 = w1[m] * link
                            k2 = w2[m] * link
                            w = x + (c1[m] * k1 + c2[m] * k2)
                            parts.append(b0[m] * w + b1[m] * k1)
                            w1[m], w2[m] = w, k1
                        while len(parts) > 1:
                            parts = [parts[i] + parts[i + 1] for i in range(0, len(parts), 2)]
                        ys[pl.ds(at, 8), :] = acc + parts[0]
                    return tuple(w1) + tuple(w2)

                zero = jnp.zeros((8, LANES), f32)
                lax.fori_loop(0, rows // 4, step, (zero,) * (2 * per))
                serve()

        def gather(r, c, s=s):
            base = pl.multiple_of(r * 16, 16)
            sq = jnp.zeros((16, LANES), f32)
            for g in range(groups):
                lanes = slice(g * LANES, (g + 1) * LANES)
                mixed = jnp.concatenate(
                    [ys[pl.ds((base + 8 * h) * groups + g, 8, stride=groups), :] for h in range(2)], axis=0)
                mb = (cur[pl.ds(base, 16), lanes].astype(f32) + mixed).astype(bf16)
                mid[pl.ds(base, 16), lanes] = mb
                mf = mb.astype(f32)
                sq = sq + mf * mf
            inv = lax.rsqrt(jnp.sum(sq, axis=1, keepdims=True) * (1.0 / width) + norm_eps)
            for g in range(groups):
                lanes = slice(g * LANES, (g + 1) * LANES)
                normed = mid[pl.ds(base, 16), lanes].astype(f32) * inv
                qs[pl.ds(base, 16), lanes] = (normed * tab_ref[s, 4 * modes + 2, g:g + 1, :]).astype(bf16)
                ks[pl.ds(base, 16), lanes] = (normed * tab_ref[s, 4 * modes + 3, g:g + 1, :]).astype(bf16)
            return c

        lax.fori_loop(0, rows // 16, gather, 0)
        serve()

        final = s == sections - 1
        together = 4
        scale = HEAD_DIM ** (-0.5) * 1.4426950408889634

        def heads(i, c, final=final):
            work = []
            for j in range(together):
                lanes = pl.ds(pl.multiple_of((i * together + j) * HEAD_DIM, HEAD_DIM), HEAD_DIM)
                for half in ((1,) if final else (0, 1)):
                    work.append((lanes, slice(half * own, (half + 1) * own), slice(0, (half + 1) * own)))
            scores = [lax.dot_general(qs[q, lanes], ks[k, lanes], (((1,), (1,)), ((), ())), preferred_element_type=f32)
                      * scale + bias[q, k] for lanes, q, k in work]
            raw = [jnp.exp2(sc - jnp.max(sc, axis=1, keepdims=True)) for sc in scores]
            weights = [(e * (1.0 / jnp.sum(e, axis=1, keepdims=True))).astype(bf16) for e in raw]
            for (lanes, q, k), wt in zip(work, weights):
                att[q, lanes] = jnp.dot(wt, mid[k, lanes], preferred_element_type=f32).astype(bf16)
            return c

        steps = width // HEAD_DIM // together
        lax.fori_loop(0, steps // 2, heads, 0)
        serve()
        lax.fori_loop(steps // 2, steps, heads, 0)
        serve(len(queue))
        arrived(s)
        if s == 0:
            mover.finish()
        cols = 256

        def project(n, c, s=s, final=final):
            lanes = pl.ds(pl.multiple_of(n * cols, cols), cols)
            r = slice(own, rows) if final else slice(0, rows)
            weight = wg[s, :, :, :, :, lanes].reshape(width, cols)
            acc = jnp.dot(att[r, :], weight, preferred_element_type=f32)
            result = (mid[r, lanes].astype(f32) + acc).astype(bf16)
            if final:
                o_ref[:, lanes] = result
            else:
                cur[:, lanes] = result
            return c

        lax.fori_loop(0, width // cols, project, 0)
    mover.finish()


def mode_table(rate, angle, coef, norm_gain, skip, gains):
    mag = jnp.exp(-rate)
    a_re, a_im = mag * jnp.cos(angle), mag * jnp.sin(angle)
    c1 = 2.0 * a_re
    c2 = -(mag * mag)
    b0 = 2.0 * coef[0]
    b1 = -2.0 * (coef[0] * a_re + coef[1] * a_im)
    return jnp.concatenate([c1, c2, b0, b1, norm_gain[None], skip[None], gains], axis=0)


def local(inputs, lengths, order, norm_gain, rate, angle, coef, skip, score_gains, out_proj):
    sections = lax.axis_size("pipe")
    rows, width = inputs.shape[1], inputs.shape[2]
    modes = rate.shape[1]
    groups = width // LANES
    table = mode_table(rate[0], angle[0], coef[0], norm_gain[0], skip[0], score_gains[0]).reshape(-1, groups, LANES)
    vm = pl.BlockSpec(memory_space=pltpu.VMEM)
    sm = pl.BlockSpec(memory_space=pltpu.SMEM)
    hb = pl.BlockSpec(memory_space=pl.ANY)
    total = 2 * rows
    moves = 128
    depth = out_proj.shape[1]
    wide = lambda: pltpu.VMEM((total, width), jnp.bfloat16)
    tall = lambda: pltpu.VMEM((total * groups, LANES), jnp.float32)
    out = pl.pallas_call(
        functools.partial(fused_kernel, width, 896, modes),
        out_shape=jax.ShapeDtypeStruct((rows, width), jnp.bfloat16),
        in_specs=[sm, vm, hb, hb, hb],
        out_specs=vm,
        scratch_shapes=[
            pltpu.VMEM((sections, YS, ZS, 2, depth, width), jnp.bfloat16),
            pltpu.VMEM((sections,) + table.shape, jnp.float32),
            wide(),
            pltpu.VMEM((sections, rows, width), jnp.bfloat16),
            tall(), tall(), wide(), wide(), wide(), wide(),
            pltpu.VMEM((total, total), jnp.float32),
            pltpu.VMEM((total * 8, LANES), jnp.float32),
            pltpu.SemaphoreType.DMA((moves,)),
            pltpu.SemaphoreType.DMA((moves,)),
            pltpu.SemaphoreType.DMA((3,)),
        ],
        compiler_params=pltpu.CompilerParams(collective_id=0, has_side_effects=True, vmem_limit_bytes=58 << 20),
        name="sections",
    )(order, lengths, out_proj[0], inputs[0], table)
    return out[None]


def solution(mesh):
    in_specs = (
        P("pipe", "seq", None),
        P(),
        P(),
        P("pipe", None),
        P("pipe", None, None),
        P("pipe", None, None),
        P("pipe", None, None, None),
        P("pipe", None),
        P("pipe", None, None),
        P("pipe", "seq", None),
    )
    out_specs = P("pipe", "seq", None)
    return jax.shard_map(local, mesh=mesh, in_specs=in_specs, out_specs=out_specs, check_vma=False)
```

```python
import functools

import jax
import jax.numpy as jnp
from jax import lax
from jax.experimental import pallas as pl
from jax.experimental.pallas import tpu as pltpu
from jax.sharding import PartitionSpec as P

HEAD_DIM = 128
LANES = 128
norm_eps = 1e-06
masked_score = -1e30


MESH = pl.DeviceIdType.MESH
ZS, YS, XS = 8, 4, 4


class Mover:
    def __init__(self, send_sems, recv_sems):
        self.send_sems, self.recv_sems, self.used, self.open = send_sems, recv_sems, 0, []

    def push(self, source, target, incoming, device):
        k = self.used
        self.used += 1
        out = pltpu.make_async_remote_copy(source, target, self.send_sems.at[k], self.recv_sems.at[k],
                                           device_id=device, device_id_type=MESH)
        out.start()
        back = pltpu.make_async_remote_copy(incoming, incoming, self.send_sems.at[k], self.recv_sems.at[k],
                                            device_id=device, device_id_type=MESH)
        self.open.append(out)
        return back.wait_recv

    def finish(self):
        for out in self.open:
            out.wait_send()
        self.open = []


def ring(mover, size, me, block, half, device, share=None):
    def at(shift):
        return lax.rem(me + (shift + size), size)
    waits = {}

    def step(t):
        def go():
            if t > 1:
                waits[t - 1, 0]()
                waits[t - 1, 1]()
            if t <= size // 2:
                pick = (lambda i, k: half(i, k)) if t == size // 2 else (lambda i, k: block(i))
                ahead, behind = at(1 - t), at(t - 1)
                waits[t, 0] = mover.push(pick(ahead, 0), pick(ahead, 0), pick(at(-t), 0), device(at(1)))
                waits[t, 1] = mover.push(pick(behind, 1), pick(behind, 1), pick(at(t), 1), device(at(-1)))
            if share is not None:
                share(at(t - 1))
                if 1 < t <= size // 2:
                    share(at(1 - t))
        return go
    return [step(t) for t in range(1, size // 2 + 2)]


def transfer_steps(mover, refs, chosen, width, split):
    w_ref, in_ref, tab_in, wg, xin, tabs, x, local_sem = refs
    pipe, seq = lax.axis_index("pipe"), lax.axis_index("seq")
    core, z, y = lax.rem(seq, 2), lax.rem(seq // 2, ZS), seq // (2 * ZS)
    rows = in_ref.shape[0]
    nseq = 2 * ZS * YS

    def seq_of(yy, zz, cc):
        return (yy * ZS + zz) * 2 + cc

    def to_x(i):
        return (i, seq)

    def to_y(i):
        return (pipe, seq_of(i, z, core))

    def to_z(i):
        return (pipe, seq_of(y, i, core))

    partner = (pipe, seq_of(y, z, 1 - core))
    following = (pipe, lax.rem(seq + 1, nseq))
    preceding = (pipe, lax.rem(seq + nseq - 1, nseq))
    peers = [to_x(lax.rem(pipe + 1, XS)), to_x(lax.rem(pipe + 3, XS)), to_y(lax.rem(y + 1, YS)), to_y(lax.rem(y + 3, YS)),
             to_z(lax.rem(z + 1, ZS)), to_z(lax.rem(z + 7, ZS)), partner, following, preceding]
    trows = tabs.shape[1] // 2
    tlow = pl.ds(core * trows, trows)
    tpart = [pl.ds(core * trows + k * (trows // 2), trows // 2) for k in range(2)]
    depth = w_ref.shape[0]

    def begin():
        bar = pltpu.get_barrier_semaphore()
        for peer in peers:
            pl.semaphore_signal(bar, inc=1, device_id=peer, device_id_type=MESH)
        pl.semaphore_wait(bar, len(peers))
        copies = [pltpu.make_async_copy(w_ref, wg.at[pipe, y, z, core], local_sem.at[0]),
                  pltpu.make_async_copy(in_ref, xin.at[pipe], local_sem.at[1]),
                  pltpu.make_async_copy(tab_in.at[tlow], tabs.at[pipe, tlow], local_sem.at[2])]
        for c in copies:
            c.start()
        for c in copies:
            c.wait()

    xw = ring(mover, XS, pipe, lambda i: wg.at[i, y, z, core],
              lambda i, k: wg.at[i, y, z, core, pl.ds(k * (depth // 2), depth // 2)], to_x)
    xi = ring(mover, XS, pipe, lambda i: xin.at[i], lambda i, k: xin.at[i, pl.ds(k * (rows // 2), rows // 2)], to_x)
    xt = ring(mover, XS, pipe, lambda i: tabs.at[i, tlow], lambda i, k: tabs.at[i, tpart[k]], to_x)
    ca, cb = pl.ds(0, split), pl.ds(split, width - split)
    held = {}

    def choose():
        x[pl.ds(rows, rows), :] = xin[chosen]
        held["halo"] = mover.push(x.at[pl.ds(rows, rows)], x.at[pl.ds(0, rows)], x.at[pl.ds(0, rows)], following)
        held["sent"] = mover.open.pop().wait_send

    def share_tables():
        other = pl.ds((1 - core) * trows, trows)
        held["tabs"] = mover.push(tabs.at[:, tlow], tabs.at[:, tlow], tabs.at[:, other], partner)

    shared = {s: [] for s in range(XS)}

    def last(s):
        yh = [pl.ds(0, YS // 2), pl.ds(YS // 2, YS // 2)]
        zh = [pl.ds(0, ZS // 2), pl.ds(ZS // 2, ZS // 2)]

        def to_partner(part):
            def share(i):
                shared[s].append(mover.push(part(i, core), part(i, core), part(i, 1 - core), partner))
            return share
        part_a = lambda i, c: wg.at[s, :, i, c, :, ca]
        part_b = lambda i, c: wg.at[s, i, :, c, :, cb]
        za = ring(mover, ZS, z, lambda i: part_a(i, core), lambda i, k: wg.at[s, yh[k], i, core, :, ca], to_z, to_partner(part_a))
        yb = ring(mover, YS, y, lambda i: part_b(i, core), lambda i, k: wg.at[s, i, zh[k], core, :, cb], to_y, to_partner(part_b))
        return za, yb

    def first(s):
        ya = ring(mover, YS, y, lambda i: wg.at[s, i, z, core, :, ca],
                  lambda i, k: wg.at[s, i, z, core, pl.ds(k * (depth // 2), depth // 2), ca], to_y)
        zb = ring(mover, ZS, z, lambda i: wg.at[s, y, i, core, :, cb],
                  lambda i, k: wg.at[s, y, i, core, pl.ds(k * (depth // 2), depth // 2), cb], to_z)
        return zb, ya

    firsts = [first(s) for s in range(XS)]
    finals = [last(s) for s in range(XS)]

    def advance(long_short, k):
        long_short[0][k - 1]()
        if k % 2:
            long_short[1][k // 2]()

    def tick(s, k):
        def go():
            advance(finals[s], k)
            if s + 1 < XS:
                advance(firsts[s + 1], k)
            if k == 5 and s + 1 < XS:
                tick(s + 1, 1)()
        return go

    def prepare(k):
        return lambda: advance(firsts[0], k)
    early = [begin, xw[0], xi[0], xw[1], xw[2], prepare(1), prepare(2), prepare(3), xi[1], xt[0], prepare(4), prepare(5),
             tick(0, 1), xi[2], choose, xt[1], tick(0, 2), xt[2], share_tables]
    ticks = [(s, tick(s, k)) for s in range(XS) for k in range(2, 6)][1:]

    def arrived(s):
        for wait in shared[s]:
            wait()
    return early, held, ticks, arrived


def document_masks(lengths_ref, chosen, first, rows, bias, links):
    f32, bf16 = jnp.float32, jnp.bfloat16
    count = lengths_ref.shape[1]
    own = rows // 2
    sizes = jnp.broadcast_to(lengths_ref[pl.ds(chosen, 1), :].astype(f32), (8, count)).astype(bf16)
    low = (lax.broadcasted_iota(jnp.int32, (count, count), 1) <= lax.broadcasted_iota(jnp.int32, (count, count), 0))
    low = low.astype(f32).astype(bf16)
    both = (((1,), (1,)), ((), ()))
    ends_row = lax.dot_general(sizes, low, both, preferred_element_type=f32)[0:1, :].astype(jnp.int32)
    ends_col = lax.dot_general(low, sizes, both, preferred_element_type=f32)[:, 0:1].astype(jnp.int32)
    index = lax.broadcasted_iota(jnp.int32, (rows, count), 0)
    down = index + first

    def doc_col(pos):
        counted = jnp.sum(jnp.where(ends_row <= pos, 1.0, 0.0), axis=1, keepdims=True)
        return jnp.where(pos[:, 0:1] >= 0, counted, -1.0)
    docs = doc_col(down)
    before = doc_col(down - 1)
    across = lax.broadcasted_iota(jnp.int32, (count, rows), 1) + first
    docs_row = jnp.sum(jnp.where(ends_col <= across, 1.0, 0.0), axis=0, keepdims=True)
    docs_row = jnp.where(across[0:1, :] >= 0, docs_row, -1.0)
    good = (docs == docs_row) & (lax.broadcasted_iota(jnp.int32, (rows, rows), 1) <= lax.broadcasted_iota(jnp.int32, (rows, rows), 0))
    bias[...] = jnp.where(good, 0.0, masked_score)
    link = jnp.where((docs == before) & (index[:, 0:1] > 0), 1.0, 0.0)
    wide = jnp.broadcast_to(link, (rows, LANES))
    for r in range(rows // 8):
        for j in range(8):
            links[pl.ds(r * 64 + j, 8, stride=8), :] = wide[r * 8:r * 8 + 8]


def fused_kernel(width, split, modes, order_ref, lengths_ref, w_ref, in_ref, tab_in, o_ref,
                 wg, tab_ref, cur, xin, xs, ys, mid, qs, ks, att, bias, links, send_sems, recv_sems, local_sem):
    sections = wg.shape[0]
    rows = cur.shape[0]
    groups = width // LANES
    halves = groups // 8
    own = rows // 2
    f32, bf16 = jnp.float32, jnp.bfloat16
    mover = Mover(send_sems, recv_sems)
    chosen = order_ref[lax.axis_index("pipe")]
    early, held, queue, arrived = transfer_steps(
        mover, (w_ref, in_ref, tab_in, wg, xin, tab_ref, cur, local_sem), chosen, width, split)
    for k, step in enumerate(early):
        step()
        if k == 3:
            document_masks(lengths_ref, chosen, (lax.axis_index("seq") - 1) * own, rows, bias, links)
    held["halo"]()
    held["tabs"]()

    def serve():
        if queue:
            queue.pop(0)[1]()

    for s in range(sections):
        def spread(r, c, s=s):
            base = pl.multiple_of(r * 16, 16)
            xb = cur[pl.ds(base, 16), :].astype(f32)
            inv = lax.rsqrt(jnp.mean(xb * xb, axis=1, keepdims=True) + norm_eps)
            for g in range(groups):
                sc = xb[:, g * LANES:(g + 1) * LANES] * inv * tab_ref[s, 4 * modes, g:g + 1, :]
                for h in range(2):
                    xs[pl.ds((base + 8 * h) * groups + g, 8, stride=groups), :] = sc[8 * h:8 * h + 8]
            return c

        lax.fori_loop(0, rows // 16, spread, 0)

        per = 8
        for hf in range(halves):
            for mg in range(modes // per):
                part = slice(8 * hf, 8 * hf + 8)
                c1 = [tab_ref[s, mg * per + m, part, :] for m in range(per)]
                c2 = [tab_ref[s, modes + mg * per + m, part, :] for m in range(per)]
                b0 = [tab_ref[s, 2 * modes + mg * per + m, part, :] for m in range(per)]
                b1 = [tab_ref[s, 3 * modes + mg * per + m, part, :] for m in range(per)]
                skip = tab_ref[s, 4 * modes + 1, part, :]

                def step(p0, state, c1=c1, c2=c2, b0=b0, b1=b1, skip=skip, hf=hf, mg=mg):
                    w1, w2 = list(state[:per]), list(state[per:])
                    for u in range(4):
                        p = p0 * 4 + u
                        at = pl.multiple_of(p * groups + 8 * hf, 8)
                        x = xs[pl.ds(at, 8), :]
                        link = links[pl.ds(pl.multiple_of(p * 8, 8), 8), :]
                        acc = skip * x if mg == 0 else ys[pl.ds(at, 8), :]
                        side = None
                        for m in range(per):
                            k1 = w1[m] * link
                            k2 = w2[m] * link
                            w = x + (c1[m] * k1 + c2[m] * k2)
                            acc = acc + b0[m] * w
                            side = b1[m] * k1 if side is None else side + b1[m] * k1
                            w1[m], w2[m] = w, k1
                        ys[pl.ds(at, 8), :] = acc + side
                    return tuple(w1) + tuple(w2)

                zero = jnp.zeros((8, LANES), f32)
                lax.fori_loop(0, rows // 4, step, (zero,) * (2 * per))
                if mg == 0:
                    serve()

        def gather(r, c, s=s):
            base = pl.multiple_of(r * 16, 16)
            sq = jnp.zeros((16, LANES), f32)
            for g in range(groups):
                lanes = slice(g * LANES, (g + 1) * LANES)
                mixed = jnp.concatenate(
                    [ys[pl.ds((base + 8 * h) * groups + g, 8, stride=groups), :] for h in range(2)], axis=0)
                mb = (cur[pl.ds(base, 16), lanes].astype(f32) + mixed).astype(bf16)
                mid[pl.ds(base, 16), lanes] = mb
                mf = mb.astype(f32)
                sq = sq + mf * mf
            inv = lax.rsqrt(jnp.sum(sq, axis=1, keepdims=True) * (1.0 / width) + norm_eps)
            for g in range(groups):
                lanes = slice(g * LANES, (g + 1) * LANES)
                normed = mid[pl.ds(base, 16), lanes].astype(f32) * inv
                qs[pl.ds(base, 16), lanes] = (normed * tab_ref[s, 4 * modes + 2, g:g + 1, :]).astype(bf16)
                ks[pl.ds(base, 16), lanes] = (normed * tab_ref[s, 4 * modes + 3, g:g + 1, :]).astype(bf16)
            return c

        lax.fori_loop(0, rows // 16, gather, 0)
        serve()

        final = s == sections - 1
        together = 4
        scale = HEAD_DIM ** (-0.5) * 1.4426950408889634

        def heads(i, c, final=final):
            work = []
            for j in range(together):
                lanes = pl.ds(pl.multiple_of((i * together + j) * HEAD_DIM, HEAD_DIM), HEAD_DIM)
                for half in ((1,) if final else (0, 1)):
                    work.append((lanes, slice(half * own, (half + 1) * own), slice(0, (half + 1) * own)))
            scores = [lax.dot_general(qs[q, lanes], ks[k, lanes], (((1,), (1,)), ((), ())), preferred_element_type=f32)
                      * scale + bias[q, k] for lanes, q, k in work]
            raw = [jnp.exp2(sc - jnp.max(sc, axis=1, keepdims=True)) for sc in scores]
            weights = [(e * (1.0 / jnp.sum(e, axis=1, keepdims=True))).astype(bf16) for e in raw]
            for (lanes, q, k), wt in zip(work, weights):
                att[q, lanes] = jnp.dot(wt, mid[k, lanes], preferred_element_type=f32).astype(bf16)
            return c

        lax.fori_loop(0, width // HEAD_DIM // together, heads, 0)
        serve()
        while queue and queue[0][0] <= s:
            serve()
        arrived(s)
        if s == 0:
            held["sent"]()
        cols = 256

        def project(n, c, s=s, final=final):
            lanes = pl.ds(pl.multiple_of(n * cols, cols), cols)
            r = slice(own, rows) if final else slice(0, rows)
            weight = wg[s, :, :, :, :, lanes].reshape(width, cols)
            acc = jnp.dot(att[r, :], weight, preferred_element_type=f32)
            result = (mid[r, lanes].astype(f32) + acc).astype(bf16)
            if final:
                o_ref[:, lanes] = result
            else:
                cur[:, lanes] = result
            return c

        lax.fori_loop(0, width // cols, project, 0)
    mover.finish()


def mode_table(rate, angle, coef, norm_gain, skip, gains):
    mag = jnp.exp(-rate)
    a_re, a_im = mag * jnp.cos(angle), mag * jnp.sin(angle)
    c1 = 2.0 * a_re
    c2 = -(mag * mag)
    b0 = 2.0 * coef[0]
    b1 = -2.0 * (coef[0] * a_re + coef[1] * a_im)
    return jnp.concatenate([c1, c2, b0, b1, norm_gain[None], skip[None], gains], axis=0)


def local(inputs, lengths, order, norm_gain, rate, angle, coef, skip, score_gains, out_proj):
    sections = lax.axis_size("pipe")
    rows, width = inputs.shape[1], inputs.shape[2]
    modes = rate.shape[1]
    groups = width // LANES
    table = mode_table(rate[0], angle[0], coef[0], norm_gain[0], skip[0], score_gains[0]).reshape(-1, groups, LANES)
    vm = pl.BlockSpec(memory_space=pltpu.VMEM)
    sm = pl.BlockSpec(memory_space=pltpu.SMEM)
    hb = pl.BlockSpec(memory_space=pl.ANY)
    total = 2 * rows
    moves = 160
    depth = out_proj.shape[1]
    wide = lambda: pltpu.VMEM((total, width), jnp.bfloat16)
    tall = lambda: pltpu.VMEM((total * groups, LANES), jnp.float32)
    out = pl.pallas_call(
        functools.partial(fused_kernel, width, 768, modes),
        out_shape=jax.ShapeDtypeStruct((rows, width), jnp.bfloat16),
        in_specs=[sm, vm, hb, hb, hb],
        out_specs=vm,
        scratch_shapes=[
            pltpu.VMEM((sections, YS, ZS, 2, depth, width), jnp.bfloat16),
            pltpu.VMEM((sections,) + table.shape, jnp.float32),
            wide(),
            pltpu.VMEM((sections, rows, width), jnp.bfloat16),
            tall(), tall(), wide(), wide(), wide(), wide(),
            pltpu.VMEM((total, total), jnp.float32),
            pltpu.VMEM((total * 8, LANES), jnp.float32),
            pltpu.SemaphoreType.DMA((moves,)),
            pltpu.SemaphoreType.DMA((moves,)),
            pltpu.SemaphoreType.DMA((3,)),
        ],
        compiler_params=pltpu.CompilerParams(collective_id=0, has_side_effects=True, vmem_limit_bytes=58 << 20),
        name="sections",
    )(order, lengths, out_proj[0], inputs[0], table)
    return out[None]


def solution(mesh):
    in_specs = (
        P("pipe", "seq", None),
        P(),
        P(),
        P("pipe", None),
        P("pipe", None, None),
        P("pipe", None, None),
        P("pipe", None, None, None),
        P("pipe", None),
        P("pipe", None, None),
        P("pipe", "seq", None),
    )
    out_specs = P("pipe", "seq", None)
    return jax.shard_map(local, mesh=mesh, in_specs=in_specs, out_specs=out_specs, check_vma=False)
```
